128 devices in a mesh: row: 8 (over z, core), col: 8 (over x, y_hi), depth: 2 (over y_lo).
Axes of the slice: x: 4, y: 4 (y_hi: 2, y_lo: 2; y = y_hi * 2 + y_lo), z: 4, core: 2. Of those that a mesh axis runs over, the one named last changes fastest.
Arguments:
- amplitudes: bfloat16 [616, 616, 1024], P('col', 'row', 'depth'), may hold values from -6 to 6
- ladder_ints: bfloat16 [616, 616, 1024], P('col', 'row', 'depth'), may hold values from -0.013671875 to 0.013671875
- cycle_ints: bfloat16 [616, 32, 2048], P('row', None, 'col'), may hold values from -0.0625 to 0.0625
- ladder_source: float32 [1024, 1024], P(('row', 'col'), 'depth'), may hold values from -6 to 6
- cycle_source: float32 [616, 32, 2048], P('col', 'depth', 'row'), may hold values from -6 to 6
- occ_energy: float32 [32], replicated, may hold values from -2 to -0.4
- virt_energy: float32 [616], replicated, may hold values from 0.2 to 3
- pair_energy: float32 [1024], P(('row', 'col')), may hold values from 0.4 to 6
- slice_energy: float32 [64], replicated, may hold values from 0.2 to 3
Outputs:
- ladder_new: float32 [1024, 1024], P(('row', 'col'), 'depth')
- cycle_new: float32 [616, 32, 2048], P('col', 'depth', 'row')
The draws below stay inside these ranges and needn't reach their ends.
All inputs are finite; a program needn't handle non-finite values.
Results may differ from the reference program's by a relative error of at most 0.0003.
Values may be sent and summed in bfloat16 or wider, within the bound.
No kernel may reach another device: no remote copies, remote signals or barrier semaphores. Data moves between devices by JAX's collectives and lax.ppermute only.
A program may use at most 128 MiB of HBM per device.

```python
import jax
import jax.numpy as jnp
from jax import lax

OCC = 32
VIRT = 616
SLICE = 64
PAIRS = 1024


def spiked(result, rng, source, target, parts, factor):
    def block_of(position):
        return (jnp.arange(result.shape[position]) // (result.shape[position] // parts)).reshape((-1,) + (1,) * (result.ndim - 1 - position))

    one_side = jax.random.permutation(rng, parts)[block_of(target)]
    far = (block_of(target) + parts // 2) % parts
    return jnp.where((block_of(source) == one_side) | (block_of(source) == far), factor * result, result)


def shard_levels(own_key, shape, shards, smallest, largest):
    loudness = 1.0
    for axis_at, blocks in shards:
        draws = jax.random.uniform(jax.random.fold_in(jax.random.fold_in(own_key, 6), axis_at), (blocks,), jnp.float32, smallest / len(shards), largest / len(shards))
        loudness = loudness * jnp.repeat(jnp.exp(draws), shape[axis_at] // blocks).reshape((-1,) + (1,) * (len(shape) - 1 - axis_at))
    return loudness


def gaussian(stream_key, shape, spread, reach, shards=(), kind=jnp.bfloat16):
    gain = shard_levels(stream_key, shape, shards, -0.22, 0.18) if shards else 1.0
    drawn = jax.random.normal(stream_key, shape, jnp.float32) * spread * gain
    return jnp.minimum(jnp.maximum(drawn, -reach), reach).astype(kind)


def noise_with(stream_key, dims, scale, limit, cuts, heavy, kind=jnp.bfloat16):
    values = scale * jax.random.normal(stream_key, dims, jnp.float32)
    if cuts:
        values = values * shard_levels(stream_key, dims, cuts, -0.22, 0.18)
    return jnp.clip(spiked(values, jax.random.fold_in(stream_key, 3), *heavy), -limit, limit).astype(kind)


def setup_inputs(seed: int = 0) -> dict:
    arg_keys = jax.random.split(jax.random.key(seed), 10)
    amplitudes = gaussian(arg_keys[0], (VIRT, VIRT, OCC * OCC), 1.0, 6.0, ((0, 8), (1, 8), (2, 2)))
    ladder_ints = noise_with(arg_keys[1], (VIRT, VIRT, PAIRS), (VIRT * VIRT) ** -0.5, 0.013671875, ((0, 8), (1, 8), (2, 2)), (1, 2, 8, 2.0))
    cycle_ints = noise_with(arg_keys[2], (VIRT, OCC, OCC * SLICE), (OCC * VIRT) ** -0.5, 0.0625, ((0, 8), (2, 8)), (0, 2, 8, 2.0))
    ladder_source = gaussian(arg_keys[3], (PAIRS, OCC * OCC), 1.0, 6.0, ((0, 64), (1, 2)), jnp.float32)
    cycle_source = gaussian(arg_keys[4], (VIRT, OCC, OCC * SLICE), 1.0, 6.0, ((0, 8), (1, 2), (2, 8)), jnp.float32)
    occ_energy = jnp.clip(jax.random.uniform(arg_keys[5], (OCC,), jnp.float32, -2.0, -0.4), -2.0, -0.4)
    virt_energy = jnp.clip(jax.random.uniform(arg_keys[6], (VIRT,), jnp.float32, 0.2, 3.0), 0.2, 3.0)
    pair_energy = jnp.clip(0.4 + 5.6 * jax.random.uniform(arg_keys[7], (PAIRS,), jnp.float32) ** shard_levels(arg_keys[7], (PAIRS,), ((0, 64),), -0.2, 0.2), 0.4, 6.0)
    slice_energy = jnp.clip(jax.random.uniform(arg_keys[8], (SLICE,), jnp.float32, 0.2, 3.0), 0.2, 3.0)
    return dict(amplitudes=amplitudes, ladder_ints=ladder_ints, cycle_ints=cycle_ints, ladder_source=ladder_source, cycle_source=cycle_source, occ_energy=occ_energy, virt_energy=virt_energy, pair_energy=pair_energy, slice_energy=slice_energy)


def reference(amplitudes, ladder_ints, cycle_ints, ladder_source, cycle_source, occ_energy, virt_energy, pair_energy, slice_energy):
    flat_amp = amplitudes.reshape(VIRT * VIRT, OCC * OCC)
    flat_slab = ladder_ints.reshape(VIRT * VIRT, PAIRS)
    ladder_sum = lax.dot_general(flat_slab, flat_amp, (((0,), (0,)), ((), ())), preferred_element_type=jnp.float32)
    occ_pairs = (occ_energy[:, None] + occ_energy[None, :]).reshape(OCC * OCC)
    ladder_den = occ_pairs[None, :] - pair_energy[:, None]
    ladder_new = (ladder_source + ladder_sum) / ladder_den
    cycle_amp = amplitudes.reshape(VIRT, VIRT, OCC, OCC).transpose(0, 2, 1, 3).reshape(VIRT * OCC, VIRT * OCC)
    cycle_mat = cycle_ints.reshape(VIRT * OCC, OCC * SLICE)
    cycle_sum = jnp.dot(cycle_amp, cycle_mat, preferred_element_type=jnp.float32).reshape(VIRT, OCC, OCC * SLICE)
    jb_part = (occ_energy[:, None] - slice_energy[None, :]).reshape(OCC * SLICE)
    cycle_den = occ_energy[None, :, None] - virt_energy[:, None, None] + jb_part[None, None, :]
    cycle_new = (cycle_source + cycle_sum) / cycle_den
    return (ladder_new, cycle_new)
```

```python
import jax
import jax.numpy as jnp
from jax import lax
from jax.experimental import pallas as pl
from jax.experimental.pallas import tpu as pltpu
from jax.sharding import PartitionSpec as P

NZ, NCORE = 4, 2
NX, NHI = 4, 2
LANES = 128
OCC = 32
SMALL = pl.CostEstimate(flops=1000, bytes_accessed=1000, transcendentals=0)
F32 = jnp.float32

SWAP_DEPTH = [(0, 1), (1, 0)]
SWAP_CORE = [(i, i ^ 1) for i in range(NZ * NCORE)]
SWAP_HI = [(i, i ^ 1) for i in range(NX * NHI)]
ACROSS = [(i, i ^ 3) for i in range(NX * NHI * 2)]


def shift_z(s):
    return [(z * NCORE + c, (z + s) % NZ * NCORE + c) for z in range(NZ) for c in range(NCORE)]


def shift_x(s):
    return [(x * NHI + h, (x + s) % NX * NHI + h) for x in range(NX) for h in range(NHI)]


def across_x(s):
    pairs = []
    for i, j in ACROSS:
        x, rest = divmod(j, NHI * 2)
        pairs.append((i, (x + s) % NX * NHI * 2 + rest))
    return pairs


def after(value, *others):
    return lax.optimization_barrier((value,) + others)[0]


def pick(value, index, axis):
    return lax.dynamic_index_in_dim(value, index, axis, keepdims=False)


def four_way(blocks, mine, axis_name, shift):
    kept = pick(blocks, mine, 0)
    got = [lax.ppermute(pick(blocks, (mine + s) % 4, 0), axis_name, shift(s)) for s in (1, 2, 3)]
    return kept + got[0] + got[1] + got[2]


def two_way(blocks, mine, axis_name, swap):
    return pick(blocks, mine, 0) + lax.ppermute(pick(blocks, 1 - mine, 0), axis_name, swap)


def reduce_col(part, x, hi):
    n, rows, pair_occ = part.shape
    keep = rows // (NX * NHI)
    v = part.reshape(n, NX, NHI, keep, pair_occ).transpose(1, 2, 0, 3, 4)
    v = four_way(v, x, "col", shift_x)
    return two_way(v, hi, "col", SWAP_HI)


def amp_kernel(src, dst, rows_in, rows_out):
    n, virt, lanes = src.shape
    occ_dev = dst.shape[1]
    per_tile = LANES // OCC
    groups = rows_in.shape[1] // per_tile
    piece = lax.broadcasted_iota(jnp.int32, (groups, LANES), 1) // OCC
    rows_in[...] = jnp.zeros_like(rows_in)

    def one(a, carry):
        for i4 in range(lanes // LANES):
            rows_in[i4, :virt, :] = src[a, :, i4 * LANES : (i4 + 1) * LANES].astype(F32)
        for i4 in range(lanes // LANES):
            v = [rows_in[i4, pl.ds(c, groups, stride=per_tile), :] for c in range(per_tile)]
            for i in range(per_tile):
                r = v[0] if i == 0 else pltpu.roll(v[0], (-i * OCC) % LANES, 1)
                for c in range(1, per_tile):
                    w = v[c] if c == i else pltpu.roll(v[c], ((c - i) * OCC) % LANES, 1)
                    r = jnp.where(piece == c, w, r)
                rows_out[pl.ds(i4 * per_tile + i, groups, stride=occ_dev), :] = r
        for g in range(groups):
            width = min(LANES, virt * OCC - g * LANES)
            tile = rows_out[g * occ_dev : (g + 1) * occ_dev, :].astype(jnp.bfloat16)
            dst[a, :, g * LANES : g * LANES + width] = tile[:, :width]
        return carry

    lax.fori_loop(0, n, one, 0)


def cycle_layout(amplitudes, occ_dev):
    virt_col, virt_row, pair_occ = amplitudes.shape
    step = 7 if virt_col % 7 == 0 else 1
    padded = pl.cdiv(virt_row * OCC, LANES) * LANES // OCC
    out = pl.pallas_call(
        amp_kernel,
        grid=(virt_col // step,),
        in_specs=[pl.BlockSpec((step, virt_row, pair_occ), lambda g: (g, 0, 0))],
        out_specs=pl.BlockSpec((step, occ_dev, virt_row * OCC), lambda g: (g, 0, 0)),
        out_shape=jax.ShapeDtypeStruct((virt_col, occ_dev, virt_row * OCC), amplitudes.dtype),
        scratch_shapes=[
            pltpu.VMEM((pair_occ // LANES, padded, LANES), F32),
            pltpu.VMEM((padded * OCC // LANES * occ_dev, LANES), F32),
        ],
        cost_estimate=SMALL,
    )(amplitudes)
    return out.reshape(virt_col * occ_dev, virt_row * OCC)


def cycle_kernel(order, amp, *refs):
    blocks, out = refs[:-1], refs[-1]
    step = pl.program_id(0)
    hi = order[1]
    for s in range(NX):

        @pl.when(step == s)
        def _():
            b = jnp.concatenate([blocks[2 * s][...], blocks[2 * s + 1][...]], axis=1)
            r = jnp.dot(amp[...], b, preferred_element_type=F32)
            out[:, pl.ds(pl.multiple_of(hi * LANES, LANES), LANES)] = r[:, :LANES]
            out[:, pl.ds(pl.multiple_of((1 - hi) * LANES, LANES), LANES)] = r[:, LANES:]


def cycle_dot(order, amp, blocks):
    m, k = amp.shape
    grid_spec = pltpu.PrefetchScalarGridSpec(
        num_scalar_prefetch=1,
        grid=(NX,),
        in_specs=[pl.BlockSpec((m, k), lambda s, o: (0, 0))]
        + [pl.BlockSpec((k, LANES), lambda s, o: (0, 0)) for _ in blocks],
        out_specs=pl.BlockSpec((m, NHI * LANES), lambda s, o: (0, (o[0] + s) % NX)),
    )
    return pl.pallas_call(
        cycle_kernel,
        grid_spec=grid_spec,
        out_shape=jax.ShapeDtypeStruct((m, NX * NHI * LANES), F32),
        compiler_params=pltpu.CompilerParams(vmem_limit_bytes=50 << 20),
        cost_estimate=SMALL,
    )(order, amp, *blocks)


def gather_near(own):
    across = lax.ppermute(own, ("col", "depth"), ACROSS)
    own_l = lax.ppermute(own, "col", shift_x(1))
    own_r = lax.ppermute(own, "col", shift_x(-1))
    own_again = after(own, own_l, own_r)
    across_l = lax.ppermute(own_again, ("col", "depth"), across_x(1))
    across_r = lax.ppermute(own_again, ("col", "depth"), across_x(-1))
    return own, across, own_l, own_r, across_l, across_r


def gather_far(near, gate):
    own, across, own_l, own_r, across_l, across_r = near
    own_far = lax.ppermute(after(own_l, gate), "col", shift_x(1))
    across_far = lax.ppermute(after(across_r, gate), "col", shift_x(-1))
    return [own, across, own_r, across_r, own_far, across_far, own_l, across_l]


def body(
    amplitudes,
    ladder_ints,
    cycle_ints,
    ladder_source,
    cycle_source,
    occ_energy,
    virt_energy,
    pair_energy,
    slice_energy,
):
    virt_col, virt_row, pair_occ = amplitudes.shape
    occ_all = occ_energy.shape[0]
    occ_dev = pair_occ // occ_all
    slice_size = slice_energy.shape[0]
    row = lax.axis_index("row")
    col = lax.axis_index("col")
    depth = lax.axis_index("depth")
    z, core = row // NCORE, row % NCORE
    x, hi = col // NHI, col % NHI

    chunks = ladder_ints.shape[2] // LANES
    got, pieces = [], []
    for c in range(chunks):
        source = ladder_ints
        if c >= 1:
            source = after(source, pieces[c - 1])
        if c >= 2:
            source = after(source, got[c - 2])
        pieces.append(lax.slice_in_dim(source, c * LANES, (c + 1) * LANES, axis=2))
        got.append(lax.ppermute(pieces[c], "depth", SWAP_DEPTH))

    halves = cycle_ints.shape[2] // LANES
    near = []
    for h in range(halves):
        source = after(cycle_ints, pieces[h], *near[h - 1][:1]) if h else after(cycle_ints, pieces[0])
        own = lax.slice_in_dim(source, h * LANES, (h + 1) * LANES, axis=2)
        near.append(gather_near(own.reshape(virt_row * occ_all, LANES)))

    def ladder_dot(ints):
        return lax.dot_general(ints, amplitudes, (((0, 1), (0, 1)), ((), ())), preferred_element_type=F32)

    own_dot = ladder_dot(ladder_ints)
    own_part = own_dot.reshape(chunks, LANES, pair_occ)

    cycle_amp = cycle_layout(amplitudes, occ_dev)
    order = jnp.stack([x, hi]).astype(jnp.int32)
    cycle_sums = []
    gate = (cycle_amp, own_dot)
    for h in range(halves):
        blocks = gather_far(near[h], gate[0])
        order = after(order, *gate, got[h], *(v for n in near for v in n[1:4]))
        part = cycle_dot(order, cycle_amp, blocks)
        gate = (part,)
        part = part.reshape(virt_col, occ_dev, NX * NHI * LANES)
        cycle_sums.append(lax.psum_scatter(part, "row", scatter_dimension=2, tiled=True))

    other = [ladder_dot(g)[None] for g in got]
    early = reduce_col(jnp.concatenate([own_part] + other[:-1], axis=0), x, hi)
    late = reduce_col(other[-1], x, hi)
    mine, rest = early[:chunks], jnp.concatenate([early[chunks:], late], axis=0)
    both = jnp.where(depth == 0, jnp.concatenate([mine, rest], 0), jnp.concatenate([rest, mine], 0))
    v = both.reshape(NZ, NCORE, both.shape[1], pair_occ).transpose(1, 0, 2, 3)
    v = two_way(v, core, "row", SWAP_CORE)
    ladder_sum = four_way(v, z, "row", shift_z)

    occ_mine = lax.dynamic_slice_in_dim(occ_energy, depth * occ_dev, occ_dev)
    occ_pairs = (occ_mine[:, None] + occ_energy[None, :]).reshape(pair_occ)
    ladder_den = occ_pairs[None, :] - pair_energy[:, None]
    ladder_new = (ladder_source + ladder_sum) / ladder_den

    cycle_sum = jnp.concatenate(cycle_sums, axis=2)
    occ_share = cycle_sum.shape[2] // slice_size
    occ_rows = lax.dynamic_slice_in_dim(occ_energy, row * occ_share, occ_share)
    virt_mine = lax.dynamic_slice_in_dim(virt_energy, col * virt_col, virt_col)
    jb_part = (occ_rows[:, None] - slice_energy[None, :]).reshape(occ_share * slice_size)
    cycle_den = occ_mine[None, :, None] - virt_mine[:, None, None] + jb_part[None, None, :]
    cycle_new = (cycle_source + cycle_sum) / cycle_den
    return (ladder_new, cycle_new)


def solution(mesh):
    placed = (
        P("col", "row", "depth"),
        P("col", "row", "depth"),
        P("row", None, "col"),
        P(("row", "col"), "depth"),
        P("col", "depth", "row"),
        P(),
        P(),
        P(("row", "col")),
        P(),
    )
    return jax.shard_map(
        body,
        mesh=mesh,
        in_specs=placed,
        out_specs=(P(("row", "col"), "depth"), P("col", "depth", "row")),
        check_vma=False,
    )
```

```python
import functools

import jax
import jax.numpy as jnp
from jax import lax
from jax.experimental import pallas as pl
from jax.experimental.pallas import tpu as pltpu
from jax.sharding import PartitionSpec as P

NZ, NCORE = 4, 2
NX, NHI = 4, 2
LANES = 128
OCC = 32
SMALL = pl.CostEstimate(flops=1000, bytes_accessed=1000, transcendentals=0)
F32 = jnp.float32

SWAP_DEPTH = [(0, 1), (1, 0)]
SWAP_CORE = [(i, i ^ 1) for i in range(NZ * NCORE)]
SWAP_HI = [(i, i ^ 1) for i in range(NX * NHI)]
ACROSS = [(i, i ^ 3) for i in range(NX * NHI * 2)]
LONG = pl.CostEstimate(flops=20_000_000_000, bytes_accessed=1000, transcendentals=0)


def shift_z(s):
    return [(z * NCORE + c, (z + s) % NZ * NCORE + c) for z in range(NZ) for c in range(NCORE)]


def shift_x(s):
    return [(x * NHI + h, (x + s) % NX * NHI + h) for x in range(NX) for h in range(NHI)]


def across_x(s):
    pairs = []
    for i, j in ACROSS:
        x, rest = divmod(j, NHI * 2)
        pairs.append((i, (x + s) % NX * NHI * 2 + rest))
    return pairs


def after(value, *others):
    return lax.optimization_barrier((value,) + others)[0]


def corner(value):
    return lax.slice(value, (0,) * value.ndim, (1,) * (value.ndim - 2) + (8, LANES))


def pick(value, index, axis):
    return lax.dynamic_index_in_dim(value, index, axis, keepdims=False)


def four_way(blocks, mine, axis_name, shift):
    kept = pick(blocks, mine, 0)
    got = [lax.ppermute(pick(blocks, (mine + s) % 4, 0), axis_name, shift(s)) for s in (1, 2, 3)]
    return kept + got[0] + got[1] + got[2]


def ring_row(keep, send, gate):
    got = {r: keep[r] + lax.ppermute(after(send[r], gate), "row", SWAP_CORE) for r in (2, 1, 3, 0)}
    half = keep.shape[1] // 2
    up = lax.ppermute(got[2][:half], "row", shift_z(1))
    down = lax.ppermute(got[2][half:], "row", shift_z(3))
    right = jnp.concatenate([got[1][:half] + up, got[1][half:]], axis=0)
    left = jnp.concatenate([got[3][:half], got[3][half:] + down], axis=0)
    below = lax.ppermute(right, "row", shift_z(1))
    above = lax.ppermute(left, "row", shift_z(3))
    return got[0] + below + above, (below, above)


def two_way(blocks, mine, axis_name, swap):
    return pick(blocks, mine, 0) + lax.ppermute(pick(blocks, 1 - mine, 0), axis_name, swap)


def turn_kernel(start, src, *refs):
    dst = refs[-src.shape[0] :]
    for s, d in enumerate(dst):
        d[...] = src[(start[0] + s) % len(dst)]


def turn(blocks, start, gates):
    n = blocks.shape[0]
    one = jax.ShapeDtypeStruct(blocks.shape[1:], blocks.dtype)
    return pl.pallas_call(
        turn_kernel,
        in_specs=[
            pl.BlockSpec(memory_space=pltpu.SMEM),
            pl.BlockSpec(memory_space=pltpu.VMEM),
        ]
        + [pl.BlockSpec(memory_space=pl.ANY)] * len(gates),
        out_specs=[pl.BlockSpec(memory_space=pltpu.VMEM)] * n,
        out_shape=[one] * n,
        cost_estimate=LONG,
    )(start.reshape(1).astype(jnp.int32), blocks, *gates)


def reduce_col(part, x, hi, gates=()):
    n, rows, pair_occ = part.shape
    keep = rows // (NX * NHI)
    v = part.reshape(n, NX, NHI, keep, pair_occ).transpose(1, 2, 0, 3, 4)
    if gates:
        kept, *sent = turn(v, x, gates)
        got = [lax.ppermute(b, "col", shift_x(s + 1)) for s, b in enumerate(sent)]
        v = kept + got[0] + got[1] + got[2]
    else:
        v = four_way(v, x, "col", shift_x)
    return two_way(v, hi, "col", SWAP_HI)


def amp_kernel(src, dst, rows_in, rows_out):
    n, virt, lanes = src.shape
    occ_dev = dst.shape[1]
    per_tile = LANES // OCC
    groups = rows_in.shape[1] // per_tile
    piece = lax.broadcasted_iota(jnp.int32, (groups, LANES), 1) // OCC
    rows_in[...] = jnp.zeros_like(rows_in)

    def one(a, carry):
        for i4 in range(lanes // LANES):
            rows_in[i4, :virt, :] = src[a, :, i4 * LANES : (i4 + 1) * LANES].astype(F32)
        for i4 in range(lanes // LANES):
            v = [rows_in[i4, pl.ds(c, groups, stride=per_tile), :] for c in range(per_tile)]
            for i in range(per_tile):
                r = v[0] if i == 0 else pltpu.roll(v[0], (-i * OCC) % LANES, 1)
                for c in range(1, per_tile):
                    w = v[c] if c == i else pltpu.roll(v[c], ((c - i) * OCC) % LANES, 1)
                    r = jnp.where(piece == c, w, r)
                rows_out[pl.ds(i4 * per_tile + i, groups, stride=occ_dev), :] = r
        for g in range(groups):
            width = min(LANES, virt * OCC - g * LANES)
            tile = rows_out[g * occ_dev : (g + 1) * occ_dev, :].astype(jnp.bfloat16)
            dst[a, :, g * LANES : g * LANES + width] = tile[:, :width]
        return carry

    lax.fori_loop(0, n, one, 0)


def cycle_layout(amplitudes, occ_dev):
    virt_col, virt_row, pair_occ = amplitudes.shape
    step = 7 if virt_col % 7 == 0 else 1
    padded = pl.cdiv(virt_row * OCC, LANES) * LANES // OCC
    out = pl.pallas_call(
        amp_kernel,
        grid=(virt_col // step,),
        in_specs=[pl.BlockSpec((step, virt_row, pair_occ), lambda g: (g, 0, 0))],
        out_specs=pl.BlockSpec((step, occ_dev, virt_row * OCC), lambda g: (g, 0, 0)),
        out_shape=jax.ShapeDtypeStruct((virt_col, occ_dev, virt_row * OCC), amplitudes.dtype),
        scratch_shapes=[
            pltpu.VMEM((pair_occ // LANES, padded, LANES), F32),
            pltpu.VMEM((padded * OCC // LANES * occ_dev, LANES), F32),
        ],
        cost_estimate=SMALL,
    )(amplitudes)
    return out.reshape(virt_col * occ_dev, virt_row * OCC)


def cycle_kernel(order, amp, *refs, blocks_in):
    blocks, (keep, send) = refs[:blocks_in], refs[-NCORE:]
    step = pl.program_id(0)
    swapped = order[1] != order[2]
    for s in range(NX):

        @pl.when(step == s)
        def _():
            for i in range(NHI):
                r = jnp.dot(amp[...], blocks[NHI * s + i][...], preferred_element_type=F32)

                @pl.when(swapped)
                def _():
                    (send, keep)[i][...] = r

                @pl.when(jnp.logical_not(swapped))
                def _():
                    (keep, send)[i][...] = r


def cycle_dot(order, amp, blocks, gates):
    m, k = amp.shape
    n = blocks[0].shape[1]
    whole = lambda s, o: (0, 0)
    once = pl.Buffered(1)
    grid_spec = pltpu.PrefetchScalarGridSpec(
        num_scalar_prefetch=1,
        grid=(NX,),
        in_specs=[pl.BlockSpec((m, k), whole, pipeline_mode=once)]
        + [pl.BlockSpec((k, n), whole, pipeline_mode=once) for _ in blocks]
        + [pl.BlockSpec(memory_space=pl.ANY) for _ in gates],
        out_specs=[pl.BlockSpec((pl.Squeezed(), m, n), lambda s, o: ((o[0] + s + NZ - o[3]) % NZ, 0, 0))] * NCORE,
    )
    return pl.pallas_call(
        functools.partial(cycle_kernel, blocks_in=len(blocks)),
        grid_spec=grid_spec,
        out_shape=[jax.ShapeDtypeStruct((NZ, m, n), F32)] * NCORE,
        compiler_params=pltpu.CompilerParams(vmem_limit_bytes=50 << 20),
        cost_estimate=SMALL,
    )(order, amp, *blocks, *gates)


def gather_cycle(own, gate):
    half = own.shape[0] // 2
    across = lax.ppermute(own, ("col", "depth"), ACROSS)
    own_l = lax.ppermute(own, "col", shift_x(1))
    own_r = lax.ppermute(own, "col", shift_x(-1))
    far_a = lax.ppermute(after(own_l, gate)[:half], "col", shift_x(1))
    far_b = lax.ppermute(after(own_r, gate)[half:], "col", shift_x(-1))
    own_far = jnp.concatenate([far_a, far_b], axis=0)
    again = after(across, far_a, far_b)
    across_l = lax.ppermute(again, "col", shift_x(1))
    across_r = lax.ppermute(again, "col", shift_x(-1))
    across_far = lax.ppermute(own_far, ("col", "depth"), ACROSS)
    return [own, across, own_r, across_r, own_far, across_far, own_l, across_l]


def body(
    amplitudes,
    ladder_ints,
    cycle_ints,
    ladder_source,
    cycle_source,
    occ_energy,
    virt_energy,
    pair_energy,
    slice_energy,
):
    virt_col, virt_row, pair_occ = amplitudes.shape
    occ_all = occ_energy.shape[0]
    occ_dev = pair_occ // occ_all
    slice_size = slice_energy.shape[0]
    row = lax.axis_index("row")
    col = lax.axis_index("col")
    depth = lax.axis_index("depth")
    z, core = row // NCORE, row % NCORE
    x, hi = col // NHI, col % NHI

    chunks = ladder_ints.shape[2] // LANES
    begun = chunks - 1
    cut = begun * LANES
    most = lax.slice_in_dim(ladder_ints, 0, cut, axis=2)
    got_most = lax.ppermute(most, "depth", SWAP_DEPTH)

    def ladder_dot(ints):
        return lax.dot_general(ints, amplitudes, (((0, 1), (0, 1)), ((), ())), preferred_element_type=F32)

    own_dot = ladder_dot(ladder_ints)
    own_part = own_dot.reshape(chunks, LANES, pair_occ)
    cycle_amp = cycle_layout(amplitudes, occ_dev)

    blocks = gather_cycle(cycle_ints.reshape(virt_row * occ_all, cycle_ints.shape[2]), corner(cycle_amp))
    last = lax.slice_in_dim(after(ladder_ints, blocks[1]), cut, chunks * LANES, axis=2)
    got_last = lax.ppermute(last, "depth", SWAP_DEPTH)
    order = jnp.stack([x, hi, core, z]).astype(jnp.int32)
    keep, send = cycle_dot(order, cycle_amp, blocks, (own_dot,))
    cycle_sum, cycle_parts = ring_row(keep, send, got_most)
    cycle_sum = cycle_sum.reshape(virt_col, occ_dev, cycle_ints.shape[2])

    most_part = ladder_dot(after(got_most, corner(keep))).reshape(begun, LANES, pair_occ)
    last_part = ladder_dot(after(got_last, *cycle_parts)).reshape(chunks - begun, LANES, pair_occ)
    early = reduce_col(jnp.concatenate([own_part, most_part], axis=0), x, hi)
    late = reduce_col(last_part, x, hi, gates=(early, *cycle_parts))
    ladder_mine, rest = early[:chunks], jnp.concatenate([early[chunks:], late], axis=0)
    both = jnp.where(depth == 0, jnp.concatenate([ladder_mine, rest], 0), jnp.concatenate([rest, ladder_mine], 0))
    v = both.reshape(NZ, NCORE, both.shape[1], pair_occ).transpose(1, 0, 2, 3)
    v = two_way(v, core, "row", SWAP_CORE)
    ladder_sum = four_way(v, z, "row", shift_z)

    occ_mine = lax.dynamic_slice_in_dim(occ_energy, depth * occ_dev, occ_dev)
    occ_pairs = (occ_mine[:, None] + occ_energy[None, :]).reshape(pair_occ)
    ladder_den = occ_pairs[None, :] - pair_energy[:, None]
    ladder_new = (ladder_source + ladder_sum) / ladder_den

    occ_share = cycle_sum.shape[2] // slice_size
    occ_rows = lax.dynamic_slice_in_dim(occ_energy, row * occ_share, occ_share)
    virt_mine = lax.dynamic_slice_in_dim(virt_energy, col * virt_col, virt_col)
    jb_part = (occ_rows[:, None] - slice_energy[None, :]).reshape(occ_share * slice_size)
    cycle_den = occ_mine[None, :, None] - virt_mine[:, None, None] + jb_part[None, None, :]
    cycle_new = (cycle_source + cycle_sum) / cycle_den
    return (ladder_new, cycle_new)


def solution(mesh):
    placed = (
        P("col", "row", "depth"),
        P("col", "row", "depth"),
        P("row", None, "col"),
        P(("row", "col"), "depth"),
        P("col", "depth", "row"),
        P(),
        P(),
        P(("row", "col")),
        P(),
    )
    return jax.shard_map(
        body,
        mesh=mesh,
        in_specs=placed,
        out_specs=(P(("row", "col"), "depth"), P("col", "depth", "row")),
        check_vma=False,
    )
```

```python
import functools

import jax
import jax.numpy as jnp
from jax import lax
from jax.experimental import pallas as pl
from jax.experimental.pallas import tpu as pltpu
from jax.sharding import PartitionSpec as P

NZ, NCORE = 4, 2
NX, NHI = 4, 2
LANES = 128
OCC = 32
SMALL = pl.CostEstimate(flops=1000, bytes_accessed=1000, transcendentals=0)
F32 = jnp.float32

SWAP_DEPTH = [(0, 1), (1, 0)]
SWAP_CORE = [(i, i ^ 1) for i in range(NZ * NCORE)]
SWAP_HI = [(i, i ^ 1) for i in range(NX * NHI)]
ACROSS = [(i, i ^ 3) for i in range(NX * NHI * 2)]
LONG = pl.CostEstimate(flops=20_000_000_000, bytes_accessed=1000, transcendentals=0)


def shift_z(s):
    return [(z * NCORE + c, (z + s) % NZ * NCORE + c) for z in range(NZ) for c in range(NCORE)]


def shift_x(s):
    return [(x * NHI + h, (x + s) % NX * NHI + h) for x in range(NX) for h in range(NHI)]


def across_x(s):
    pairs = []
    for i, j in ACROSS:
        x, rest = divmod(j, NHI * 2)
        pairs.append((i, (x + s) % NX * NHI * 2 + rest))
    return pairs


def after(value, *others):
    return lax.optimization_barrier((value,) + others)[0]


def corner(value):
    return lax.slice(value, (0,) * value.ndim, (1,) * (value.ndim - 2) + (8, LANES))


def pick(value, index, axis):
    return lax.dynamic_index_in_dim(value, index, axis, keepdims=False)


def four_way(blocks, mine, axis_name, shift):
    kept = pick(blocks, mine, 0)
    got = [lax.ppermute(pick(blocks, (mine + s) % 4, 0), axis_name, shift(s)) for s in (1, 2, 3)]
    return kept + got[0] + got[1] + got[2]


def swap_add(keep, send):
    return [a + lax.ppermute(b, "row", SWAP_CORE) for a, b in zip(keep, send)]


def up_z(value):
    return lax.ppermute(value, "row", shift_z(1))


def down_z(value):
    return lax.ppermute(value, "row", shift_z(3))


def two_way(blocks, mine, axis_name, swap):
    return pick(blocks, mine, 0) + lax.ppermute(pick(blocks, 1 - mine, 0), axis_name, swap)


def turn_kernel(start, src, *refs):
    dst = refs[-src.shape[1] :]
    for s, d in enumerate(dst):
        d[...] = src[:, (start[0] + s) % len(dst)]


def turn(blocks, start, gates, cost):
    n = blocks.shape[1]
    one = jax.ShapeDtypeStruct(blocks.shape[:1] + blocks.shape[2:], blocks.dtype)
    return pl.pallas_call(
        turn_kernel,
        in_specs=[
            pl.BlockSpec(memory_space=pltpu.SMEM),
            pl.BlockSpec(memory_space=pltpu.VMEM),
        ]
        + [pl.BlockSpec(memory_space=pl.ANY)] * len(gates),
        out_specs=[pl.BlockSpec(memory_space=pltpu.VMEM)] * n,
        out_shape=[one] * n,
        cost_estimate=cost,
    )(start.reshape(1).astype(jnp.int32), blocks, *gates)


def reduce_col(part, x, hi, gates, cost):
    n, rows, pair_occ = part.shape
    keep = rows // (NX * NHI)
    kept, *sent = turn(part.reshape(n, NX, NHI, keep, pair_occ), x, gates, cost)
    got = [lax.ppermute(b, "col", shift_x(s + 1)) for s, b in enumerate(sent)]
    v = kept + got[0] + got[1] + got[2]
    return pick(v, hi, 1) + lax.ppermute(pick(v, 1 - hi, 1), "col", SWAP_HI)


def amp_kernel(src, dst, rows_in, rows_out):
    n, virt, lanes = src.shape
    occ_dev = dst.shape[1]
    per_tile = LANES // OCC
    groups = rows_in.shape[1] // per_tile
    piece = lax.broadcasted_iota(jnp.int32, (groups, LANES), 1) // OCC
    rows_in[...] = jnp.zeros_like(rows_in)

    def one(a, carry):
        for i4 in range(lanes // LANES):
            rows_in[i4, :virt, :] = src[a, :, i4 * LANES : (i4 + 1) * LANES].astype(F32)
        for i4 in range(lanes // LANES):
            v = [rows_in[i4, pl.ds(c, groups, stride=per_tile), :] for c in range(per_tile)]
            for i in range(per_tile):
                r = v[0] if i == 0 else pltpu.roll(v[0], (-i * OCC) % LANES, 1)
                for c in range(1, per_tile):
                    w = v[c] if c == i else pltpu.roll(v[c], ((c - i) * OCC) % LANES, 1)
                    r = jnp.where(piece == c, w, r)
                rows_out[pl.ds(i4 * per_tile + i, groups, stride=occ_dev), :] = r
        for g in range(groups):
            width = min(LANES, virt * OCC - g * LANES)
            tile = rows_out[g * occ_dev : (g + 1) * occ_dev, :].astype(jnp.bfloat16)
            dst[a, :, g * LANES : g * LANES + width] = tile[:, :width]
        return carry

    lax.fori_loop(0, n, one, 0)


def cycle_layout(amplitudes, occ_dev):
    virt_col, virt_row, pair_occ = amplitudes.shape
    step = 7 if virt_col % 7 == 0 else 1
    padded = pl.cdiv(virt_row * OCC, LANES) * LANES // OCC
    out = pl.pallas_call(
        amp_kernel,
        grid=(virt_col // step,),
        in_specs=[pl.BlockSpec((step, virt_row, pair_occ), lambda g: (g, 0, 0))],
        out_specs=pl.BlockSpec((step, occ_dev, virt_row * OCC), lambda g: (g, 0, 0)),
        out_shape=jax.ShapeDtypeStruct((virt_col, occ_dev, virt_row * OCC), amplitudes.dtype),
        scratch_shapes=[
            pltpu.VMEM((pair_occ // LANES, padded, LANES), F32),
            pltpu.VMEM((padded * OCC // LANES * occ_dev, LANES), F32),
        ],
        cost_estimate=SMALL,
    )(amplitudes)
    return out.reshape(virt_col * occ_dev, virt_row * OCC)


def cycle_kernel(order, amp, *refs, chips, blocks_in):
    count = NCORE * len(chips)
    blocks, outs = refs[:blocks_in], refs[-2 * count - 6 : -6]
    amp_buf, buf, res, amp_sems, sems, out_sems = refs[-6:]
    x, hi, core, z = order[0], order[1], order[2], order[3]
    swapped = hi != core
    half = amp.shape[0] // 2
    amp_in = [
        pltpu.make_async_copy(amp.at[pl.ds(i * half, half)], amp_buf.at[pl.ds(i * half, half)], amp_sems.at[i])
        for i in range(2)
    ]
    amp_in[0].start()
    copies = []
    width = buf.shape[2] // NCORE
    for n, r in enumerate(chips):
        s = (z + r + NX - x) % NX
        for other in range(NCORE):
            columns = buf.at[n, :, pl.ds(other * width, width)]
            copies.append(pltpu.make_async_copy(blocks[0], columns, sems.at[n, other]))
            for k in range(blocks_in):
                block, near = divmod(k, NHI)
                here = (s == block) & (swapped == bool(near ^ other))

                @pl.when(here)
                def _():
                    pltpu.make_async_copy(blocks[k], columns, sems.at[n, other]).start()

        if n == 0:
            amp_in[1].start()

    writes = {}
    for n in range(len(chips)):
        for copy in copies[NCORE * n : NCORE * (n + 1)]:
            copy.wait()
        for i in range(2):
            if n == 0:
                amp_in[i].wait()
            else:
                for write in writes[n - 1, i]:
                    write.wait()
            res[i] = jnp.dot(amp_buf[i * half : (i + 1) * half], buf[n], preferred_element_type=F32)
            writes[n, i] = [
                pltpu.make_async_copy(
                    res.at[i, :, pl.ds(other * width, width)], outs[2 * (NCORE * n + other) + i], out_sems.at[i, other]
                )
                for other in range(NCORE)
            ]
            for write in writes[n, i]:
                write.start()
    for i in range(2):
        for write in writes[len(chips) - 1, i]:
            write.wait()


def cycle_dot(order, amp, blocks, chips, gates):
    m, k = amp.shape
    n = blocks[0].shape[1]
    count = NCORE * len(chips)
    out = pl.pallas_call(
        functools.partial(cycle_kernel, chips=chips, blocks_in=len(blocks)),
        in_specs=[pl.BlockSpec(memory_space=pltpu.SMEM)] + [pl.BlockSpec(memory_space=pl.ANY)] * (1 + len(blocks) + len(gates)),
        out_specs=[pl.BlockSpec(memory_space=pl.ANY)] * (2 * count),
        out_shape=[jax.ShapeDtypeStruct((m // 2, n), F32)] * (2 * count),
        scratch_shapes=[
            pltpu.VMEM((m, k), amp.dtype),
            pltpu.VMEM((len(chips), k, NCORE * n), amp.dtype),
            pltpu.VMEM((2, m // 2, NCORE * n), F32),
            pltpu.SemaphoreType.DMA((2,)),
            pltpu.SemaphoreType.DMA((len(chips), NCORE)),
            pltpu.SemaphoreType.DMA((2, NCORE)),
        ],
        compiler_params=pltpu.CompilerParams(vmem_limit_bytes=50 << 20),
        cost_estimate=SMALL,
    )(order, amp, *blocks, *gates)
    return {r: (out[4 * i : 4 * i + 2], out[4 * i + 2 : 4 * i + 4]) for i, r in enumerate(chips)}


def gather_cycle(own, gate):
    half = own.shape[0] // 2
    across = lax.ppermute(own, ("col", "depth"), ACROSS)
    own_l = lax.ppermute(own, "col", shift_x(1))
    own_r = lax.ppermute(own, "col", shift_x(-1))
    far_a = lax.ppermute(after(own_l, gate)[:half], "col", shift_x(1))
    far_b = lax.ppermute(after(own_r, gate)[half:], "col", shift_x(-1))
    own_far = jnp.concatenate([far_a, far_b], axis=0)
    again = after(across, far_a, far_b)
    across_l = lax.ppermute(again, "col", shift_x(1))
    across_r = lax.ppermute(again, "col", shift_x(-1))
    across_far = lax.ppermute(own_far, ("col", "depth"), ACROSS)
    return [own, across, own_r, across_r, own_far, across_far, own_l, across_l]


def body(
    amplitudes,
    ladder_ints,
    cycle_ints,
    ladder_source,
    cycle_source,
    occ_energy,
    virt_energy,
    pair_energy,
    slice_energy,
):
    virt_col, virt_row, pair_occ = amplitudes.shape
    occ_all = occ_energy.shape[0]
    occ_dev = pair_occ // occ_all
    slice_size = slice_energy.shape[0]
    row = lax.axis_index("row")
    col = lax.axis_index("col")
    depth = lax.axis_index("depth")
    z, core = row // NCORE, row % NCORE
    x, hi = col // NHI, col % NHI

    chunks = ladder_ints.shape[2] // LANES
    begun = chunks // 2
    cut = begun * LANES
    most = lax.slice_in_dim(ladder_ints, 0, cut, axis=2)
    got_most = lax.ppermute(most, "depth", SWAP_DEPTH)

    def ladder_dot(ints):
        return lax.dot_general(ints, amplitudes, (((0, 1), (0, 1)), ((), ())), preferred_element_type=F32)

    own_dot = ladder_dot(ladder_ints)
    own_part = own_dot.reshape(chunks, LANES, pair_occ)
    cycle_amp = cycle_layout(amplitudes, occ_dev)

    blocks = gather_cycle(cycle_ints.reshape(virt_row * occ_all, cycle_ints.shape[2]), corner(cycle_amp))
    last = lax.slice_in_dim(after(ladder_ints, blocks[1]), cut, chunks * LANES, axis=2)
    got_last = lax.ppermute(last, "depth", SWAP_DEPTH)
    order = jnp.stack([x, hi, core, z]).astype(jnp.int32)
    parts = cycle_dot(order, cycle_amp, blocks, (2, 1, 3, 0), (own_dot, got_most))
    far = swap_add(*parts[2])
    up, down = up_z(far[0]), down_z(far[1])
    right, left = swap_add(*parts[1]), swap_add(*parts[3])
    right_rest, left_rest = up_z(right[1]), down_z(left[0])
    below, above = up_z(right[0] + up), down_z(left[1] + down)
    mine = swap_add(*parts[0])
    cycle_sum = jnp.concatenate([mine[0] + below + left_rest, mine[1] + right_rest + above], axis=0)
    cycle_sum = cycle_sum.reshape(virt_col, occ_dev, cycle_ints.shape[2])

    most_part = ladder_dot(got_most).reshape(begun, LANES, pair_occ)
    last_part = ladder_dot(got_last).reshape(chunks - begun, LANES, pair_occ)
    early = reduce_col(jnp.concatenate([own_part, most_part], axis=0), x, hi, (up, down, right[1], left[0]), SMALL)
    late = reduce_col(last_part, x, hi, (early, below, above, right_rest, left_rest), LONG)
    ladder_mine, rest = early[:chunks], jnp.concatenate([early[chunks:], late], axis=0)
    both = jnp.where(depth == 0, jnp.concatenate([ladder_mine, rest], 0), jnp.concatenate([rest, ladder_mine], 0))
    v = both.reshape(NZ, NCORE, both.shape[1], pair_occ).transpose(1, 0, 2, 3)
    v = two_way(v, core, "row", SWAP_CORE)
    ladder_sum = four_way(v, z, "row", shift_z)

    occ_mine = lax.dynamic_slice_in_dim(occ_energy, depth * occ_dev, occ_dev)
    occ_pairs = (occ_mine[:, None] + occ_energy[None, :]).reshape(pair_occ)
    ladder_den = occ_pairs[None, :] - pair_energy[:, None]
    ladder_new = (ladder_source + ladder_sum) / ladder_den

    occ_share = cycle_sum.shape[2] // slice_size
    occ_rows = lax.dynamic_slice_in_dim(occ_energy, row * occ_share, occ_share)
    virt_mine = lax.dynamic_slice_in_dim(virt_energy, col * virt_col, virt_col)
    jb_part = (occ_rows[:, None] - slice_energy[None, :]).reshape(occ_share * slice_size)
    cycle_den = occ_mine[None, :, None] - virt_mine[:, None, None] + jb_part[None, None, :]
    cycle_new = (cycle_source + cycle_sum) / cycle_den
    return (ladder_new, cycle_new)


def solution(mesh):
    placed = (
        P("col", "row", "depth"),
        P("col", "row", "depth"),
        P("row", None, "col"),
        P(("row", "col"), "depth"),
        P("col", "depth", "row"),
        P(),
        P(),
        P(("row", "col")),
        P(),
    )
    return jax.shard_map(
        body,
        mesh=mesh,
        in_specs=placed,
        out_specs=(P(("row", "col"), "depth"), P("col", "depth", "row")),
        check_vma=False,
    )
```
